32 devices in a mesh: dp: 16 (over z, x, core), tensor: 2 (over y).
Axes of the slice: x: 2, y: 2, z: 4, core: 2. Of those that a mesh axis runs over, the one named last changes fastest.
Arguments:
- tokens: bfloat16 [8192, 1024], P('dp'), may hold values from -6 to 6
- segment_ids: int32 [16, 512], P('dp'), may hold values from 0 to 2, as said below
- mixer_gain: float32 [1024], replicated, may hold values from 0.25 to 1.75
- query_weight: bfloat16 [1024, 1024], P(None, 'tensor'), may hold values from -0.1875 to 0.1875
- key_weight: bfloat16 [1024, 1024], P(None, 'tensor'), may hold values from -0.1875 to 0.1875
- value_weight: bfloat16 [1024, 2048], P(None, 'tensor'), may hold values from -0.1875 to 0.1875
- gate_weight: bfloat16 [1024, 2048], P(None, 'tensor'), may hold values from -0.1875 to 0.1875
- beta_weight: bfloat16 [1024, 8], P(None, 'tensor'), may hold values from -0.1875 to 0.1875
- decay_weight: bfloat16 [1024, 8], P(None, 'tensor'), may hold values from -0.1875 to 0.1875
- query_conv: float32 [4, 1024], P(None, 'tensor'), may hold values from -3 to 3
- key_conv: float32 [4, 1024], P(None, 'tensor'), may hold values from -3 to 3
- value_conv: float32 [4, 2048], P(None, 'tensor'), may hold values from -3 to 3
- decay_log: float32 [8], P('tensor'), may hold values from -7 to -3
- decay_bias: float32 [8], P('tensor'), may hold values from -1.5 to 1.5
- output_gain: float32 [256], replicated, may hold values from 0.25 to 1.75
- out_weight: bfloat16 [2048, 1024], P('tensor'), may hold values from -0.25 to 0.25
- feed_gain: float32 [1024], replicated, may hold values from 0.25 to 1.75
- feed_gate: bfloat16 [1024, 2816], P(None, 'tensor'), may hold values from -0.1875 to 0.1875
- feed_up: bfloat16 [1024, 2816], P(None, 'tensor'), may hold values from -0.1875 to 0.1875
- feed_down: bfloat16 [2816, 1024], P('tensor'), may hold values from -0.21875 to 0.21875
- cotangent: bfloat16 [8192, 1024], P(('dp', 'tensor')), may hold values from -6 to 6
Outputs:
- block_out: bfloat16 [8192, 1024], P(('dp', 'tensor'))
- tokens_grad: bfloat16 [8192, 1024], P(('dp', 'tensor'))
- mixer_gain_grad: float32 [1024], replicated
- query_weight_grad: float32 [1024, 1024], P('dp', 'tensor')
- key_weight_grad: float32 [1024, 1024], P('dp', 'tensor')
- value_weight_grad: float32 [1024, 2048], P('dp', 'tensor')
- gate_weight_grad: float32 [1024, 2048], P('dp', 'tensor')
- beta_weight_grad: float32 [1024, 8], P('dp', 'tensor')
- decay_weight_grad: float32 [1024, 8], P('dp', 'tensor')
- query_conv_grad: float32 [4, 1024], P(None, 'tensor')
- key_conv_grad: float32 [4, 1024], P(None, 'tensor')
- value_conv_grad: float32 [4, 2048], P(None, 'tensor')
- decay_log_grad: float32 [8], P('tensor')
- decay_bias_grad: float32 [8], P('tensor')
- output_gain_grad: float32 [256], replicated
- out_weight_grad: float32 [2048, 1024], P('tensor', 'dp')
- feed_gain_grad: float32 [1024], replicated
- feed_gate_grad: float32 [1024, 2816], P('dp', 'tensor')
- feed_up_grad: float32 [1024, 2816], P('dp', 'tensor')
- feed_down_grad: float32 [2816, 1024], P('tensor', 'dp')
The draws below stay inside these ranges and needn't reach their ends.
Inputs may be any that keep to these rules, and one draw needn't show every extreme that they name: `segment_ids`: in each of the 16 rows the id is 0 at the first token, never falls, and rises by one at each document start; every row holds two or three documents.
All inputs are finite; a program needn't handle non-finite values.
Results may differ from the reference program's by a relative error of at most 0.017.
Values may be sent and summed in bfloat16 or wider, within the bound.
A program may use at most 256 MiB of HBM per device.

```python
import jax
import jax.numpy as jnp
from jax import lax

D = 1024
HEADS = 8
DK = 128
DV = 256
KERNEL = 4
FF = 2816
BLOCK = 64
LEN = 512
SEQS = 16
TOKENS = 8192


def draw_segment_ids(key, part):
    keys_all = jax.random.split(key, 4)
    rows_shape = (SEQS, 1)
    first_any = jax.random.randint(keys_all[0], rows_shape, 1, LEN)
    first_lead = jax.random.randint(keys_all[1], rows_shape, 1, LEN // 5)
    second_any = jax.random.randint(keys_all[2], rows_shape, 2 * LEN // 5, 4 * LEN)
    second_lead = jax.random.randint(keys_all[3], rows_shape, 2 * LEN // 5, 3 * LEN // 5)
    row_number = lax.broadcasted_iota(jnp.int32, rows_shape, 0)
    leading = row_number == 0
    first_doc = jnp.where(leading, first_lead, first_any)
    second_doc = jnp.where(leading, second_lead, second_any)
    position = lax.broadcasted_iota(jnp.int32, (SEQS, LEN), 1)
    labels = (position >= first_doc).astype(jnp.int32)
    labels = labels + (position >= first_doc + second_doc).astype(jnp.int32)
    return labels


def raised(drawn, stream_key, source, target, blocks, factor):
    def block_of(dim):
        return (jnp.arange(drawn.shape[dim]) // (drawn.shape[dim] // blocks)).reshape((-1,) + (1,) * (drawn.ndim - 1 - dim))

    near = jax.random.permutation(stream_key, blocks)[block_of(target)]
    other_side = (block_of(target) + blocks // 2) % blocks
    return jnp.where((block_of(source) == near) | (block_of(source) == other_side), factor * drawn, drawn)


def block_scale(rng, extent, cuts, low, high):
    loudness, own = 1.0, jax.random.fold_in(rng, 6)
    for axis_at, parts in cuts:
        steps = jnp.exp(jax.random.uniform(jax.random.fold_in(own, axis_at), (parts,), jnp.float32, low / len(cuts), high / len(cuts)))
        loudness = loudness * jnp.repeat(steps, extent[axis_at] // parts).reshape([-1 if axis == axis_at else 1 for axis in range(len(extent))])
    return loudness


def normal_values(rng, dims, scale, limit, shards=(), dtype=jnp.bfloat16):
    values = jax.random.normal(rng, dims, jnp.float32) * scale
    if len(shards) > 0:
        values = block_scale(rng, dims, shards, -0.22, 0.18) * values
    return jnp.clip(values, min=-limit, max=limit).astype(dtype)


def heavy_noise(key, shape, scale, bound, shards, heavy, dtype=jnp.bfloat16):
    entries = scale * jax.random.normal(key, shape, jnp.float32)
    if shards:
        entries = entries * block_scale(key, shape, shards, -0.22, 0.18)
    return jnp.clip(raised(entries, jax.random.fold_in(key, 3), *heavy), -bound, bound).astype(dtype)


def setup_inputs(seed: int = 0) -> dict:
    seeds = jax.random.split(jax.random.key(seed), 22)
    tokens = heavy_noise(seeds[0], (TOKENS, D), 1.0, 6.0, ((0, 16),), (0, 1, 16, 2.0))
    segment_ids = draw_segment_ids(jax.random.fold_in(seeds[21], 71), 0)
    mixer_gain = jnp.clip(1.0 + 0.15 * jax.random.normal(seeds[2], (D,), jnp.float32), 0.25, 1.75)
    query_weight = normal_values(seeds[3], (D, HEADS * DK), D ** -0.5, 0.1875, ((1, 2),))
    key_weight = normal_values(seeds[4], (D, HEADS * DK), D ** -0.5, 0.1875, ((1, 2),))
    value_weight = normal_values(seeds[5], (D, HEADS * DV), D ** -0.5, 0.1875, ((1, 2),))
    gate_weight = normal_values(seeds[6], (D, HEADS * DV), D ** -0.5, 0.1875, ((1, 2),))
    beta_weight = normal_values(seeds[7], (D, HEADS), D ** -0.5, 0.1875, ((1, 2),))
    decay_weight = normal_values(seeds[8], (D, HEADS), D ** -0.5, 0.1875, ((1, 2),))
    query_conv = normal_values(seeds[9], (KERNEL, HEADS * DK), KERNEL ** -0.5, 3.0, ((1, 2),), jnp.float32)
    key_conv = normal_values(seeds[10], (KERNEL, HEADS * DK), KERNEL ** -0.5, 3.0, ((1, 2),), jnp.float32)
    value_conv = normal_values(seeds[11], (KERNEL, HEADS * DV), KERNEL ** -0.5, 3.0, ((1, 2),), jnp.float32)
    decay_log = jnp.clip(-7.0 + 4.0 * jax.random.uniform(seeds[12], (HEADS,), jnp.float32) ** block_scale(seeds[12], (HEADS,), ((0, 2),), -0.2, 0.2), -7.0, -3.0)
    decay_bias = jnp.clip(jax.random.uniform(seeds[13], (HEADS,), jnp.float32, -1.5, 1.5) * block_scale(seeds[13], (HEADS,), ((0, 2),), -0.4, 0.0), -1.5, 1.5)
    output_gain = jnp.clip(1.0 + 0.15 * jax.random.normal(seeds[14], (DV,), jnp.float32), 0.25, 1.75)
    out_weight = normal_values(seeds[15], (HEADS * DV, D), (HEADS * DV // 4) ** -0.5, 0.25, ((0, 2),))
    feed_gain = jnp.clip(1.0 + 0.15 * jax.random.normal(seeds[16], (D,), jnp.float32), 0.25, 1.75)
    feed_gate = normal_values(seeds[17], (D, FF), D ** -0.5, 0.1875, ((1, 2),))
    feed_up = normal_values(seeds[18], (D, FF), D ** -0.5, 0.1875, ((1, 2),))
    feed_down = normal_values(seeds[19], (FF, D), (FF // 4) ** -0.5, 0.21875, ((0, 2),))
    cotangent = heavy_noise(seeds[20], (TOKENS, D), 1.0, 6.0, ((0, 32),), (0, 1, 32, 2.75))
    return {"tokens": tokens, "segment_ids": segment_ids, "mixer_gain": mixer_gain, "query_weight": query_weight, "key_weight": key_weight, "value_weight": value_weight, "gate_weight": gate_weight, "beta_weight": beta_weight, "decay_weight": decay_weight, "query_conv": query_conv, "key_conv": key_conv, "value_conv": value_conv, "decay_log": decay_log, "decay_bias": decay_bias, "output_gain": output_gain, "out_weight": out_weight, "feed_gain": feed_gain, "feed_gate": feed_gate, "feed_up": feed_up, "feed_down": feed_down, "cotangent": cotangent}


EPSILON = 1e-06
PRECISE = lax.Precision.HIGHEST

def norm_forward(values, gain_row):
    factor = lax.rsqrt(lax.optimization_barrier(jnp.mean(values * values, axis=-1, keepdims=True)) + EPSILON)
    return (values * factor * gain_row, factor)

def norm_backward(upstream, values, factor, gain_row):
    unit_scaled = values * factor
    weighted = upstream * gain_row
    backward = factor * (weighted - unit_scaled * lax.optimization_barrier(jnp.mean(weighted * unit_scaled, axis=-1, keepdims=True)))
    return (backward, upstream * unit_scaled)

def silu_slope(argument):
    logistic = jax.nn.sigmoid(argument)
    return logistic * (1.0 + argument * (1.0 - logistic))

def dot_first(left, right):
    return lax.dot_general(left.astype(jnp.float32), right.astype(jnp.float32), (((0,), (0,)), ((), ())), preferred_element_type=jnp.float32)

def dot_last(left, right):
    return lax.dot_general(left.astype(jnp.float32), right.astype(jnp.float32), (((1,), (1,)), ((), ())), preferred_element_type=jnp.float32)

def same_mask(segments, taps):
    length = segments.shape[1]
    columns = []
    for offset in range(taps):
        shifted = jnp.pad(segments, ((0, 0), (offset, 0)), constant_values=-1)[:, :length]
        columns.append((shifted == segments).astype(jnp.float32))
    return jnp.stack(columns, axis=-1)

def short_conv(values, weight, live_mask):
    length = values.shape[1]
    summed = values * weight[0] * live_mask[..., 0:1]
    for offset in range(1, weight.shape[0]):
        shifted = jnp.pad(values, ((0, 0), (offset, 0), (0, 0)))[:, :length]
        summed = summed + shifted * weight[offset] * live_mask[..., offset:offset + 1]
    return summed

def delta_rule(queries, key_vecs, values, beta_rate, log_decay, segments, block_size):
    seq_count, length, head_count, key_dim = queries.shape
    value_dim = values.shape[-1]
    block_count = length // block_size

    def blocks(source):
        shaped = source.reshape((seq_count, block_count, block_size) + source.shape[2:])
        return jnp.moveaxis(shaped, 1, 0)
    segment_blocks = blocks(segments.astype(jnp.int32))
    previous = jnp.concatenate([jnp.full((1, seq_count), -1, jnp.int32), segment_blocks[:-1, :, block_size - 1]], axis=0)
    row_index = lax.broadcasted_iota(jnp.int32, (block_size, block_size), 0)
    col_index = lax.broadcasted_iota(jnp.int32, (block_size, block_size), 1)
    inclusive = row_index >= col_index
    strictly = row_index > col_index

    def advance(memory, inputs):
        query_block, key_block, value_block, beta_block, decay_block, seg_block, prev_block = inputs
        query_heads = jnp.moveaxis(query_block, 2, 1)
        key_heads = jnp.moveaxis(key_block, 2, 1)
        value_heads = jnp.moveaxis(value_block, 2, 1)
        beta_heads = jnp.moveaxis(beta_block, 2, 1)
        cumulative = jnp.cumsum(jnp.moveaxis(decay_block, 2, 1), axis=-1)
        same_doc = (seg_block[:, :, None] == seg_block[:, None, :])[:, None]
        keep_mask = jnp.logical_and(inclusive, same_doc)
        spread = cumulative[..., :, None] - cumulative[..., None, :]
        within = jnp.where(keep_mask, jnp.exp(jnp.where(keep_mask, spread, 0.0)), 0.0)
        fresh_mask = (seg_block == prev_block[:, None])[:, None, :]
        start_decay = jnp.where(fresh_mask, jnp.exp(cumulative), 0.0)
        last_seg = seg_block[:, block_size - 1]
        tail_mask = (seg_block == last_seg[:, None])[:, None, :]
        end_decay = jnp.where(tail_mask, jnp.exp(cumulative[..., block_size - 1:] - cumulative), 0.0)
        carried = jnp.where((last_seg == prev_block)[:, None], jnp.exp(cumulative[..., block_size - 1]), 0.0)
        key_gram = jnp.einsum('bhid,bhjd->bhij', key_heads, key_heads, precision=PRECISE)
        lower_part = jnp.where(strictly, key_gram * within, 0.0) * beta_heads[..., None]
        recalled = jnp.einsum('bhid,bhde->bhie', key_heads, memory, precision=PRECISE)
        target = beta_heads[..., None] * (value_heads - start_decay[..., None] * recalled)
        update = jax.scipy.linalg.solve_triangular(lower_part, target, lower=True, unit_diagonal=True)
        scores = jnp.einsum('bhid,bhjd->bhij', query_heads, key_heads, precision=PRECISE) * within
        output = start_decay[..., None] * jnp.einsum('bhid,bhde->bhie', query_heads, memory, precision=PRECISE)
        output = output + jnp.einsum('bhij,bhje->bhie', scores, update, precision=PRECISE)
        memory = carried[..., None, None] * memory + jnp.einsum('bhjd,bhje->bhde', key_heads * end_decay[..., None], update, precision=PRECISE)
        return (memory, output)
    initial = jnp.zeros((seq_count, head_count, key_dim, value_dim), jnp.float32)
    final_memory, outputs = lax.scan(advance, initial, (blocks(queries), blocks(key_vecs), blocks(values), blocks(beta_rate), blocks(log_decay), segment_blocks, previous))
    return jnp.transpose(outputs, (1, 0, 3, 2, 4)).reshape(seq_count, length, head_count, value_dim)

def mixer_local(query_pre, key_pre, value_pre, gate_pre, beta_pre, decay_pre, query_conv, key_conv, value_conv, decay_log, decay_bias, output_gain, segments, key_dim, block_size):
    seq_count, length = segments.shape
    head_count = decay_log.shape[0]
    value_dim = output_gain.shape[0]
    live_mask = same_mask(segments, query_conv.shape[0])
    queries = jax.nn.silu(short_conv(query_pre, query_conv, live_mask)).reshape(seq_count, length, head_count, key_dim)
    queries = queries * lax.rsqrt(lax.optimization_barrier(jnp.sum(queries * queries, axis=-1, keepdims=True)) + EPSILON) * key_dim ** (-0.5)
    key_vecs = jax.nn.silu(short_conv(key_pre, key_conv, live_mask)).reshape(seq_count, length, head_count, key_dim)
    key_vecs = key_vecs * lax.rsqrt(lax.optimization_barrier(jnp.sum(key_vecs * key_vecs, axis=-1, keepdims=True)) + EPSILON)
    values = jax.nn.silu(short_conv(value_pre, value_conv, live_mask)).reshape(seq_count, length, head_count, value_dim)
    beta_rate = jax.nn.sigmoid(beta_pre)
    log_decay = -jnp.exp(decay_log) * jax.nn.softplus(decay_pre + decay_bias)
    recurrent = delta_rule(queries, key_vecs, values, beta_rate, log_decay, segments, block_size)
    normed = recurrent * lax.rsqrt(lax.optimization_barrier(jnp.mean(recurrent * recurrent, axis=-1, keepdims=True)) + EPSILON)
    gated_out = normed * output_gain * jax.nn.silu(gate_pre.reshape(seq_count, length, head_count, value_dim))
    return gated_out.reshape(seq_count, length, head_count * value_dim)

def reference(tokens, segment_ids, mixer_gain, query_weight, key_weight, value_weight, gate_weight, beta_weight, decay_weight, query_conv, key_conv, value_conv, decay_log, decay_bias, output_gain, out_weight, feed_gain, feed_gate, feed_up, feed_down, cotangent):
    seq_total, length = segment_ids.shape
    feature_count = tokens.shape[1]
    token_seqs = tokens.reshape(seq_total, length, feature_count)
    cotangent_seqs = cotangent.reshape(seq_total, length, feature_count)
    projections = (query_weight, key_weight, value_weight, gate_weight, beta_weight, decay_weight)
    key_dim = query_weight.shape[1] // decay_log.shape[0]
    shapes = (mixer_gain.shape, query_weight.shape, key_weight.shape, value_weight.shape, gate_weight.shape, beta_weight.shape, decay_weight.shape, query_conv.shape, key_conv.shape, value_conv.shape, decay_log.shape, decay_bias.shape, output_gain.shape, out_weight.shape, feed_gain.shape, feed_gate.shape, feed_up.shape, feed_down.shape)

    def one_sequence(totals, inputs):
        token_rows, segment_row, cotangent_rows = inputs
        segments = segment_row[None].astype(jnp.int32)
        inputs_float = token_rows.astype(jnp.float32)
        normed_first, factor_first = norm_forward(inputs_float, mixer_gain)
        normed_in = normed_first.astype(jnp.bfloat16)
        projected = [jnp.dot(normed_in.astype(jnp.float32), weight.astype(jnp.float32), preferred_element_type=jnp.float32).reshape(1, length, -1) for weight in projections]

        def mixer_apply(*members):
            return mixer_local(*members, segments, key_dim, BLOCK)
        gated_out, mixer_back = jax.vjp(mixer_apply, *projected, query_conv, key_conv, value_conv, decay_log, decay_bias, output_gain)
        gated_low = gated_out.reshape(length, -1).astype(jnp.bfloat16)
        middle = inputs_float + jnp.dot(gated_low.astype(jnp.float32), out_weight.astype(jnp.float32), preferred_element_type=jnp.float32)
        normed_second, factor_second = norm_forward(middle, feed_gain)
        normed_mid = normed_second.astype(jnp.bfloat16)
        swish_in = jnp.dot(normed_mid.astype(jnp.float32), feed_gate.astype(jnp.float32), preferred_element_type=jnp.float32)
        linear_up = jnp.dot(normed_mid.astype(jnp.float32), feed_up.astype(jnp.float32), preferred_element_type=jnp.float32)
        hidden = (jax.nn.silu(swish_in) * linear_up).astype(jnp.bfloat16)
        block_rows = (middle + jnp.dot(hidden.astype(jnp.float32), feed_down.astype(jnp.float32), preferred_element_type=jnp.float32)).astype(jnp.bfloat16)
        downward_grad = dot_first(hidden, cotangent_rows)
        grad_hidden = dot_last(cotangent_rows, feed_down)
        swish_grad = (grad_hidden * linear_up * silu_slope(swish_in)).astype(jnp.bfloat16)
        linear_grad = (grad_hidden * jax.nn.silu(swish_in)).astype(jnp.bfloat16)
        gating_grad = dot_first(normed_mid, swish_grad)
        upward_grad = dot_first(normed_mid, linear_grad)
        grad_second = dot_last(swish_grad, feed_gate) + dot_last(linear_grad, feed_up)
        back_second, second_terms = norm_backward(grad_second, middle, factor_second, feed_gain)
        gain_second = lax.optimization_barrier(jnp.sum(second_terms, axis=0))
        grad_middle = cotangent_rows.astype(jnp.float32) + back_second
        grad_middle_low = grad_middle.astype(jnp.bfloat16)
        outward_grad = dot_first(gated_low, grad_middle_low)
        grad_gated = dot_last(grad_middle_low, out_weight)
        mixer_grads = mixer_back(grad_gated.reshape(1, length, -1))
        low_grads = [member.reshape(length, -1).astype(jnp.bfloat16) for member in mixer_grads[:6]]
        proj_grads = [dot_first(normed_in, member) for member in low_grads]
        grad_first = dot_last(low_grads[0], projections[0])
        for index_proj in range(1, 6):
            grad_first = grad_first + dot_last(low_grads[index_proj], projections[index_proj])
        back_first, first_terms = norm_backward(grad_first, inputs_float, factor_first, mixer_gain)
        gain_first = lax.optimization_barrier(jnp.sum(first_terms, axis=0))
        grad_rows = (grad_middle + back_first).astype(jnp.bfloat16)
        step_grads = (gain_first, proj_grads[0], proj_grads[1], proj_grads[2], proj_grads[3], proj_grads[4], proj_grads[5], mixer_grads[6], mixer_grads[7], mixer_grads[8], mixer_grads[9], mixer_grads[10], mixer_grads[11], outward_grad, gain_second, gating_grad, upward_grad, downward_grad)
        updated = tuple((older + newer for older, newer in zip(totals, step_grads)))
        return (updated, (block_rows, grad_rows))
    initial = tuple((jnp.zeros(shape_one, jnp.float32) for shape_one in shapes))
    totals, results = lax.scan(one_sequence, initial, (token_seqs, segment_ids, cotangent_seqs))
    block_out = results[0].reshape(seq_total * length, feature_count)
    tokens_grad = results[1].reshape(seq_total * length, feature_count)
    return (block_out, tokens_grad, totals[0], totals[1], totals[2], totals[3], totals[4], totals[5], totals[6], totals[7], totals[8], totals[9], totals[10], totals[11], totals[12], totals[13], totals[14], totals[15], totals[16], totals[17])
```

```python
import functools

import jax
import jax.numpy as jnp
from jax import lax
from jax.experimental import pallas as pl
from jax.experimental.pallas import tpu as pltpu
from jax.sharding import PartitionSpec as P

CHUNK = 256
EPSILON = 1e-06
F32 = jnp.float32
BF16 = jnp.bfloat16

NN = (((1,), (0,)), ((), ()))
NT = (((1,), (1,)), ((), ()))
TN = (((0,), (0,)), ((), ()))


def split(value):
    high = value.astype(BF16)
    return high, (value - high.astype(F32)).astype(BF16)


def mm(left, right, dims):
    dot = functools.partial(lax.dot_general, dimension_numbers=dims, preferred_element_type=F32)
    return dot(left[0], right[0]) + (dot(left[0], right[1]) + dot(left[1], right[0]))


def iotas(rows, columns):
    return (
        lax.broadcasted_iota(jnp.int32, (rows, columns), 0),
        lax.broadcasted_iota(jnp.int32, (rows, columns), 1),
    )


def to_column(row, eye):
    return jnp.sum(jnp.where(eye, row, 0.0), axis=1, keepdims=True)


def to_row(column, eye):
    return jnp.sum(jnp.where(eye, column, 0.0), axis=0, keepdims=True)


def live_masks(segment_column, taps):
    length = segment_column.shape[0]
    wide = jnp.broadcast_to(segment_column, (length, 128))
    rows, _ = iotas(length, 128)
    masks = [None]
    for tap in range(1, taps):
        same = jnp.logical_and(pltpu.roll(wide, tap, 0) == wide, rows >= tap)
        masks.append(jnp.where(same, 1.0, 0.0))
    return masks


def widen(mask, width):
    return jnp.concatenate([mask] * (width // 128), axis=1) if width > 128 else mask


def conv_forward(pre, weight, masks):
    total = pre * weight[0:1]
    for tap in range(1, len(masks)):
        mask = widen(masks[tap], pre.shape[1])
        total = total + pltpu.roll(pre, tap, 0) * mask * weight[tap : tap + 1]
    return total


def conv_backward(upstream, pre, weight, masks):
    length = pre.shape[0]
    back = upstream * weight[0:1]
    weight_rows = [jnp.sum(upstream * pre, axis=0, keepdims=True)]
    for tap in range(1, len(masks)):
        masked = upstream * widen(masks[tap], pre.shape[1])
        back = back + pltpu.roll(masked, length - tap, 0) * weight[tap : tap + 1]
        weight_rows.append(jnp.sum(masked * pltpu.roll(pre, tap, 0), axis=0, keepdims=True))
    return back, jnp.concatenate(weight_rows, axis=0)


def slope(argument, logistic):
    return logistic * (1.0 + argument * (1.0 - logistic))


def unit_rows(values):
    return lax.rsqrt(jnp.sum(values * values, axis=1, keepdims=True) + EPSILON)


def chunk_decays(seg_row, cum_row, at, size, eye):
    rows, cols = iotas(size, size)
    seg = seg_row[:, at : at + size]
    cum = cum_row[:, at : at + size]
    seg_col, cum_col = to_column(seg, eye), to_column(cum, eye)
    keep = jnp.logical_and(rows >= cols, seg_col == seg)
    within = jnp.where(keep, jnp.exp(jnp.where(keep, cum_col - cum, 0.0)), 0.0)
    last_seg, last_cum = seg[:, size - 1 :], cum[:, size - 1 :]
    end = jnp.where(seg_col == last_seg, jnp.exp(last_cum - cum_col), 0.0)
    if at == 0:
        return within, end, None, None
    prev_seg = seg_row[:, at - 1 : at]
    start = jnp.where(seg_col == prev_seg, jnp.exp(cum_col), 0.0)
    carried = jnp.where(last_seg == prev_seg, jnp.exp(last_cum), 0.0)
    return within, end, start, carried


def invert_unit_lower(lower, size):
    rows, cols = iotas(size, size)
    inverse = jnp.where(rows == cols, 1.0, 0.0)
    shift = 0
    while (1 << shift) < size:
        pair = lax.shift_right_logical(rows, shift + 1) == lax.shift_right_logical(cols, shift + 1)
        odd = jnp.bitwise_and(lax.shift_right_logical(rows, shift), 1) == 1
        even = jnp.bitwise_and(lax.shift_right_logical(cols, shift), 1) == 0
        part = jnp.where(jnp.logical_and(pair, jnp.logical_and(odd, even)), lower, 0.0)
        if shift == 0:
            inverse = inverse - part
        else:
            both = split(inverse)
            inverse = inverse - mm(split(mm(both, split(part), NN)), both, NN)
        shift += 1
    return inverse


def forward_kernel(
    chunk, seg_ref, cum_ref, beta_ref, qp_ref, kp_ref, vp_ref, gp_ref, qw_ref, kw_ref, vw_ref,
    og_ref, gated_ref, rec_ref, upd_ref, inv_ref, mem_ref,
):
    length, key_dim = qp_ref.shape
    rows, cols = iotas(chunk, chunk)
    eye = rows == cols
    seg_row, cum_row, beta_row = seg_ref[...], cum_ref[0], beta_ref[0]
    seg_col = jnp.concatenate(
        [to_column(seg_row[:, at : at + chunk], eye) for at in range(0, length, chunk)], axis=0
    )
    masks = live_masks(seg_col, qw_ref.shape[0])

    def silu_conv(pre_ref, weight_ref):
        summed = conv_forward(pre_ref[...], weight_ref[...], masks)
        return summed * jax.nn.sigmoid(summed)

    queries = silu_conv(qp_ref, qw_ref)
    queries = queries * unit_rows(queries) * key_dim ** (-0.5)
    keys = silu_conv(kp_ref, kw_ref)
    keys = keys * unit_rows(keys)
    values = silu_conv(vp_ref, vw_ref)
    gain = og_ref[...]
    memory = None
    for at in range(0, length, chunk):
        here = slice(at, at + chunk)
        within, end, start, carried = chunk_decays(seg_row, cum_row, at, chunk, eye)
        beta = to_column(beta_row[:, here], eye)
        query, key = split(queries[here]), split(keys[here])
        lower = jnp.where(rows > cols, mm(key, key, NT) * within, 0.0) * beta
        inverse = invert_unit_lower(lower, chunk)
        target = values[here]
        if memory is not None:
            mem = split(memory)
            target = target - start * mm(key, mem, NN)
            mem_ref[0, at // chunk * key_dim : (at // chunk + 1) * key_dim, :] = memory
        else:
            mem_ref[0, 0:key_dim, :] = jnp.zeros_like(mem_ref[0, 0:key_dim, :])
        update = mm(split(inverse), split(beta * target), NN)
        upd = split(update)
        scores = mm(query, key, NT) * within
        output = mm(split(scores), upd, NN)
        if memory is not None:
            output = output + start * mm(query, mem, NN)
        if at + chunk < length:
            grown = mm(split(keys[here] * end), upd, TN)
            memory = grown if memory is None else carried * memory + grown
        factor = lax.rsqrt(jnp.mean(output * output, axis=1, keepdims=True) + EPSILON)
        gate = gp_ref[here, :]
        gated_ref[here, :] = (
            output * factor * gain * (gate * jax.nn.sigmoid(gate))
        ).astype(BF16)
        rec_ref[here, :] = output
        upd_ref[here, :] = update
        inv_ref[0, here, :] = inverse


def backward_kernel(
    chunk, seg_ref, cum_ref, beta_ref, qp_ref, kp_ref, vp_ref, gp_ref, qw_ref, kw_ref, vw_ref,
    og_ref, rec_ref, upd_ref, inv_ref, mem_ref, up_ref,
    dq_ref, dk_ref, dv_ref, dg_ref, dqw_ref, dkw_ref, dvw_ref, dog_ref, dbeta_ref, dcum_ref,
    query_scr, key_scr, value_scr,
):
    length, key_dim = qp_ref.shape
    scale = key_dim ** (-0.5)
    rows, cols = iotas(chunk, chunk)
    eye = rows == cols
    seg_row, cum_row, beta_row = seg_ref[...], cum_ref[0], beta_ref[0]
    seg_col = jnp.concatenate(
        [to_column(seg_row[:, at : at + chunk], eye) for at in range(0, length, chunk)], axis=0
    )
    masks = live_masks(seg_col, qw_ref.shape[0])
    query_sum = conv_forward(qp_ref[...], qw_ref[...], masks)
    key_sum = conv_forward(kp_ref[...], kw_ref[...], masks)
    value_sum = conv_forward(vp_ref[...], vw_ref[...], masks)
    query_sig, key_sig = jax.nn.sigmoid(query_sum), jax.nn.sigmoid(key_sum)
    value_sig = jax.nn.sigmoid(value_sum)
    query_act, key_act = query_sum * query_sig, key_sum * key_sig
    query_norm, key_norm = unit_rows(query_act), unit_rows(key_act)
    queries = query_act * query_norm * scale
    keys = key_act * key_norm
    values = value_sum * value_sig
    gain = og_ref[...]
    gain_grad = jnp.zeros_like(gain)
    grad_memory = None
    for at in reversed(range(0, length, chunk)):
        here = slice(at, at + chunk)
        index = at // chunk
        output, gate, up = rec_ref[here, :], gp_ref[here, :], up_ref[here, :]
        factor = lax.rsqrt(jnp.mean(output * output, axis=1, keepdims=True) + EPSILON)
        gate_sig = jax.nn.sigmoid(gate)
        normed = output * factor
        silu_gate = gate * gate_sig
        dg_ref[here, :] = (up * normed * gain * slope(gate, gate_sig)).astype(BF16)
        gain_grad = gain_grad + jnp.sum(up * normed * silu_gate, axis=0, keepdims=True)
        weighted = up * gain * silu_gate
        grad_out = factor * (
            weighted - normed * jnp.mean(weighted * normed, axis=1, keepdims=True)
        )
        within, end, start, carried = chunk_decays(seg_row, cum_row, at, chunk, eye)
        beta = to_column(beta_row[:, here], eye)
        query_f, key_f = queries[here], keys[here]
        query, key = split(query_f), split(key_f)
        update = upd_ref[here, :]
        upd = split(update)
        gram = jnp.where(rows > cols, mm(key, key, NT) * within, 0.0)
        scores = mm(query, key, NT) * within
        grad_o = split(grad_out)
        grad_update = mm(split(scores), grad_o, TN)
        if grad_memory is not None:
            grad_mem = split(grad_memory)
            grad_update = grad_update + mm(split(key_f * end), grad_mem, NN)
        grad_target = mm(split(inv_ref[0, here, :]), split(grad_update), TN)
        grad_scores = mm(grad_o, upd, NT)
        grad_lower = jnp.where(rows > cols, -mm(split(grad_target), upd, NT), 0.0)
        residual = values[here]
        grad_resid = beta * grad_target
        spread = grad_scores * scores + grad_lower * gram * beta
        cum_column = jnp.sum(spread, axis=1, keepdims=True)
        cum_line = -jnp.sum(spread, axis=0, keepdims=True)
        grad_prod = split(grad_scores * within)
        grad_gram = split(grad_lower * within * beta)
        grad_query = mm(grad_prod, key, NN)
        grad_key = mm(grad_prod, query, TN) + mm(grad_gram, key, NN) + mm(grad_gram, key, TN)
        new_grad_memory = None
        if at > 0:
            memory = mem_ref[0, index * key_dim : (index + 1) * key_dim, :]
            mem = split(memory)
            key_mem, query_mem = mm(key, mem, NN), mm(query, mem, NN)
            residual = residual - start * key_mem
            start_out, start_res = start * grad_out, start * grad_resid
            cum_column = cum_column + jnp.sum(
                start_out * query_mem - start_res * key_mem, axis=1, keepdims=True
            )
            start_o, start_r = split(start_out), split(start_res)
            grad_query = grad_query + mm(start_o, mem, NT)
            grad_key = grad_key - mm(start_r, mem, NT)
            new_grad_memory = mm(query, start_o, TN) - mm(key, start_r, TN)
        beta_grad = jnp.sum(grad_target * residual, axis=1, keepdims=True) + jnp.sum(
            grad_lower * gram, axis=1, keepdims=True
        )
        if grad_memory is not None:
            tail = end * mm(upd, grad_mem, NT)
            grad_key = grad_key + tail
            tail_rows = jnp.sum(tail * key_f, axis=1, keepdims=True)
            cum_column = cum_column - tail_rows
            last = jnp.sum(tail_rows, axis=0, keepdims=True)
            if at > 0:
                last = last + carried * jnp.sum(
                    jnp.sum(grad_memory * memory, axis=1, keepdims=True), axis=0, keepdims=True
                )
                new_grad_memory = new_grad_memory + carried * grad_memory
            cum_line = cum_line + jnp.where(cols[0:1] == chunk - 1, last, 0.0)
        grad_memory = new_grad_memory
        dcum_ref[0, :, here] = cum_line + to_row(cum_column, eye)
        dbeta_ref[0, :, here] = to_row(beta_grad, eye)
        query_scr[here, :] = grad_query
        key_scr[here, :] = grad_key
        value_scr[here, :] = grad_resid
    dog_ref[0] = gain_grad
    grad_query, grad_key = query_scr[...], key_scr[...]
    grad_query = (scale * query_norm) * (
        grad_query
        - query_act
        * (query_norm * query_norm * jnp.sum(grad_query * query_act, axis=1, keepdims=True))
    )
    grad_key = key_norm * (
        grad_key
        - key_act * (key_norm * key_norm * jnp.sum(grad_key * key_act, axis=1, keepdims=True))
    )
    back, dqw_ref[...] = conv_backward(
        grad_query * slope(query_sum, query_sig), qp_ref[...], qw_ref[...], masks
    )
    dq_ref[...] = back.astype(BF16)
    back, dkw_ref[...] = conv_backward(
        grad_key * slope(key_sum, key_sig), kp_ref[...], kw_ref[...], masks
    )
    dk_ref[...] = back.astype(BF16)
    back, dvw_ref[...] = conv_backward(
        value_scr[...] * slope(value_sum, value_sig), vp_ref[...], vw_ref[...], masks
    )
    dv_ref[...] = back.astype(BF16)


class Mixer:
    def __init__(self, length, heads, key_dim, value_dim, taps):
        self.chunk = min(CHUNK, length)
        self.length, self.heads = length, heads
        self.key_dim, self.value_dim, self.taps = key_dim, value_dim, taps
        chunks = length // self.chunk
        self.whole = pl.BlockSpec((1, length), lambda h: (0, 0))
        self.line = pl.BlockSpec((1, 1, length), lambda h: (h, 0, 0))
        self.narrow = pl.BlockSpec((length, key_dim), lambda h: (0, h))
        self.wide = pl.BlockSpec((length, value_dim), lambda h: (0, h))
        self.narrow_taps = pl.BlockSpec((taps, key_dim), lambda h: (0, h))
        self.wide_taps = pl.BlockSpec((taps, value_dim), lambda h: (0, h))
        self.gain = pl.BlockSpec((1, value_dim), lambda h: (0, 0))
        self.gain_out = pl.BlockSpec((1, 1, value_dim), lambda h: (h, 0, 0))
        self.inverse = pl.BlockSpec((1, length, self.chunk), lambda h: (h, 0, 0))
        self.memory = pl.BlockSpec((1, chunks * key_dim, value_dim), lambda h: (h, 0, 0))
        self.chunks = chunks
        self.inputs = (
            [self.whole] + [self.line] * 2 + [self.narrow] * 2 + [self.wide] * 2
            + [self.narrow_taps] * 2 + [self.wide_taps, self.gain]
        )
        self.params = pltpu.CompilerParams(
            dimension_semantics=("arbitrary",), vmem_limit_bytes=56 << 20
        )

    def cost(self, products):
        flops = 2 * self.heads * self.chunks * products * 3 * self.chunk**3
        return pl.CostEstimate(
            flops=flops,
            transcendentals=self.heads * self.length * 2048,
            bytes_accessed=self.heads * self.length * 1600 * 4,
        )

    def forward(self, *arguments):
        length, heads, values = self.length, self.heads, self.heads * self.value_dim
        return pl.pallas_call(
            functools.partial(forward_kernel, self.chunk),
            grid=(heads,),
            in_specs=self.inputs,
            out_specs=[self.wide] * 3 + [self.inverse, self.memory],
            out_shape=[
                jax.ShapeDtypeStruct((length, values), BF16),
                jax.ShapeDtypeStruct((length, values), F32),
                jax.ShapeDtypeStruct((length, values), F32),
                jax.ShapeDtypeStruct((heads, length, self.chunk), F32),
                jax.ShapeDtypeStruct((heads, self.chunks * self.key_dim, self.value_dim), F32),
            ],
            compiler_params=self.params,
            cost_estimate=self.cost(20),
            name="mixer_forward",
        )(*arguments)

    def backward(self, *arguments):
        length, heads = self.length, self.heads
        keys, values = heads * self.key_dim, heads * self.value_dim
        return pl.pallas_call(
            functools.partial(backward_kernel, self.chunk),
            grid=(heads,),
            in_specs=self.inputs + [self.wide] * 2 + [self.inverse, self.memory, self.wide],
            out_specs=[self.narrow] * 2 + [self.wide] * 2 + [self.narrow_taps] * 2
            + [self.wide_taps, self.gain_out] + [self.line] * 2,
            out_shape=[
                jax.ShapeDtypeStruct((length, keys), BF16),
                jax.ShapeDtypeStruct((length, keys), BF16),
                jax.ShapeDtypeStruct((length, values), BF16),
                jax.ShapeDtypeStruct((length, values), BF16),
                jax.ShapeDtypeStruct((self.taps, keys), F32),
                jax.ShapeDtypeStruct((self.taps, keys), F32),
                jax.ShapeDtypeStruct((self.taps, values), F32),
                jax.ShapeDtypeStruct((heads, 1, self.value_dim), F32),
                jax.ShapeDtypeStruct((heads, 1, length), F32),
                jax.ShapeDtypeStruct((heads, 1, length), F32),
            ],
            scratch_shapes=[
                pltpu.VMEM((length, self.key_dim), F32),
                pltpu.VMEM((length, self.key_dim), F32),
                pltpu.VMEM((length, self.value_dim), F32),
            ],
            compiler_params=self.params,
            cost_estimate=self.cost(14),
            name="mixer_backward",
        )(*arguments)


def swapped(value, axis, bit):
    count = lax.axis_size(axis)
    return lax.ppermute(value, axis, [(i, i ^ (1 << bit)) for i in range(count)])


def axis_bits(axis):
    count = lax.axis_size(axis)
    bits = count.bit_length() - 1
    assert count == 1 << bits, "axis size"
    return bits


def scatter_rows(value, axis, order):
    bits = axis_bits(axis)
    index = lax.axis_index(axis)
    rows = value.shape[0] >> bits
    value = value.reshape((2,) * bits + (rows,) + value.shape[1:])
    left = list(range(bits - 1, -1, -1))
    for step, bit in enumerate(order):
        dim = left.index(bit)
        mine = jnp.bitwise_and(lax.shift_right_logical(index, bit), 1)
        keep = lax.dynamic_index_in_dim(value, mine, dim, keepdims=False)
        send = lax.dynamic_index_in_dim(value, 1 - mine, dim, keepdims=False)
        value = keep.astype(F32) + swapped(send, axis, bit).astype(F32)
        if step + 1 < bits:
            value = value.astype(BF16)
        left.pop(dim)
    return value


def all_sum(value, axis):
    for bit in range(axis_bits(axis)):
        value = value + swapped(value, axis, bit)
    return value


def all_sum_low(value, axis):
    for bit in range(axis_bits(axis)):
        low = value.astype(BF16)
        value = low.astype(F32) + swapped(low, axis, bit).astype(F32)
    return value


def dot(left, right, dims=NN, out=F32):
    return lax.dot_general(left, right, dims, preferred_element_type=out)


def per_device(
    tokens, segment_ids, mixer_gain, query_weight, key_weight, value_weight, gate_weight,
    beta_weight, decay_weight, query_conv, key_conv, value_conv, decay_log, decay_bias,
    output_gain, out_weight, feed_gain, feed_gate, feed_up, feed_down, cotangent,
):
    seq_count, length = segment_ids.shape
    assert seq_count == 1
    heads, value_dim = decay_log.shape[0], output_gain.shape[0]
    key_dim = query_weight.shape[1] // heads
    tensor_bits = axis_bits("tensor")
    tensor_order = list(range(tensor_bits - 1, -1, -1))
    share = length >> tensor_bits
    first_row = lax.axis_index("tensor") * share

    def my_rows(value):
        return lax.dynamic_slice_in_dim(value, first_row, share, 0)

    mixer = Mixer(length, heads, key_dim, value_dim, query_conv.shape[0])
    chunk = mixer.chunk
    cotangent_all = lax.all_gather(cotangent, "tensor", axis=0, tiled=True)
    inputs = tokens.astype(F32)
    factor_first = lax.rsqrt(jnp.mean(inputs * inputs, axis=-1, keepdims=True) + EPSILON)
    normed_in = (inputs * factor_first * mixer_gain).astype(BF16)
    query_pre, key_pre = dot(normed_in, query_weight), dot(normed_in, key_weight)
    value_pre, gate_pre = dot(normed_in, value_weight), dot(normed_in, gate_weight)
    small_weight = jnp.concatenate([beta_weight, decay_weight], axis=1)
    small_pre = dot(small_weight, normed_in, (((0,), (1,)), ((), ())))

    def rates(small, log, bias):
        beta = jax.nn.sigmoid(small[:heads])
        log_decay = -jnp.exp(log)[:, None] * jax.nn.softplus(small[heads:] + bias[:, None])
        summed = jnp.cumsum(log_decay.reshape(heads, length // chunk, chunk), axis=-1)
        return summed.reshape(heads, 1, length), beta.reshape(heads, 1, length)

    (cum, beta), rates_back = jax.vjp(rates, small_pre, decay_log, decay_bias)
    shared = (
        segment_ids.astype(F32), cum, beta, query_pre, key_pre, value_pre, gate_pre,
        query_conv, key_conv, value_conv, output_gain[None],
    )
    gated, recurrent, update, inverse, memory = mixer.forward(*shared)
    middle = inputs + all_sum_low(dot(gated, out_weight), "tensor")
    factor_second = lax.rsqrt(jnp.mean(middle * middle, axis=-1, keepdims=True) + EPSILON)
    normed_mid = (middle * factor_second * feed_gain).astype(BF16)
    swish_in, linear_up = dot(normed_mid, feed_gate), dot(normed_mid, feed_up)
    grad_hidden = dot(cotangent_all, feed_down, NT)
    logistic = jax.nn.sigmoid(swish_in)
    swish = swish_in * logistic
    hidden = (swish * linear_up).astype(BF16)
    swish_grad = (grad_hidden * linear_up * slope(swish_in, logistic)).astype(BF16)
    linear_grad = (grad_hidden * swish).astype(BF16)
    second_part = dot(swish_grad, feed_gate, NT) + dot(linear_grad, feed_up, NT)
    grad_second = all_sum_low(second_part, "tensor")
    feed_part = dot(hidden, feed_down, out=BF16)
    feed_rows = scatter_rows(feed_part, "tensor", tensor_order)
    block_out = (my_rows(middle) + feed_rows).astype(BF16)

    def norm_backward(upstream, values, factor, gain):
        unit = values * factor
        weighted = upstream * gain
        mean = jnp.mean(weighted * unit, axis=-1, keepdims=True)
        return factor * (weighted - unit * mean), upstream * unit

    dp_bits = axis_bits("dp")
    across = [0] + [bit for bit in (1, 2, 3) if bit < dp_bits] + list(range(4, dp_bits))
    along = [0] + list(range(2, dp_bits)) + ([1] if dp_bits > 1 else [])
    if dp_bits == 0:
        across = along = []
    gate_sum = scatter_rows(dot(normed_mid, swish_grad, TN, BF16), "dp", across)
    up_sum = scatter_rows(dot(normed_mid, linear_grad, TN, BF16), "dp", along)
    down_sum = scatter_rows(dot(cotangent_all, hidden, TN, BF16), "dp", across)

    back_second, second_terms = norm_backward(grad_second, middle, factor_second, feed_gain)
    gain_second = jnp.sum(my_rows(second_terms), axis=0)
    grad_middle = cotangent_all.astype(F32) + back_second
    grad_middle_low = grad_middle.astype(BF16)
    grad_gated = dot(grad_middle_low, out_weight, NT)
    out_sum = scatter_rows(dot(grad_middle_low, gated, TN, BF16), "dp", along)

    (
        low_query, low_key, low_value, low_gate, query_taps, key_taps, value_taps, gain_heads,
        beta_rows, cum_rows,
    ) = mixer.backward(*shared, recurrent, update, inverse, memory, grad_gated)
    small_grad, log_grad, bias_grad = rates_back((cum_rows, beta_rows))
    low_small = small_grad.astype(BF16)
    first_part = (
        dot(low_query, query_weight, NT)
        + dot(low_key, key_weight, NT)
        + dot(low_value, value_weight, NT)
        + dot(low_gate, gate_weight, NT)
        + dot(low_small, small_weight, (((0,), (1,)), ((), ())))
    )
    grad_first = scatter_rows(first_part.astype(BF16), "tensor", tensor_order)
    value_sum = scatter_rows(dot(normed_in, low_value, TN, BF16), "dp", across)
    gate_proj_sum = scatter_rows(dot(normed_in, low_gate, TN, BF16), "dp", along)
    query_sum = scatter_rows(dot(normed_in, low_query, TN, BF16), "dp", across)
    key_sum = scatter_rows(dot(normed_in, low_key, TN, BF16), "dp", along)
    small_sum = scatter_rows(
        dot(normed_in, low_small, (((0,), (1,)), ((), ())), BF16), "dp", across
    )
    back_first, first_terms = norm_backward(
        grad_first, my_rows(inputs), my_rows(factor_first), mixer_gain
    )
    tokens_grad = (my_rows(grad_middle) + back_first).astype(BF16)

    gains = [jnp.sum(first_terms, axis=0), gain_second, jnp.sum(gain_heads, axis=(0, 1))]
    taps = [query_taps.reshape(-1), key_taps.reshape(-1), value_taps.reshape(-1)]
    own = taps + [log_grad, bias_grad]
    gains_sum = all_sum(jnp.concatenate(gains), "tensor")
    packed = all_sum(jnp.concatenate([gains_sum] + own), "dp")
    sums, place = [], 0
    for piece in gains + own:
        sums.append(packed[place : place + piece.shape[0]])
        place += piece.shape[0]
    return (
        block_out,
        tokens_grad,
        sums[0],
        query_sum,
        key_sum,
        value_sum,
        gate_proj_sum,
        small_sum[:, :heads],
        small_sum[:, heads:],
        sums[3].reshape(query_conv.shape),
        sums[4].reshape(key_conv.shape),
        sums[5].reshape(value_conv.shape),
        sums[6],
        sums[7],
        sums[2],
        out_sum.T,
        sums[1],
        gate_sum,
        up_sum,
        down_sum.T,
    )


def solution(mesh):
    rows, both = P("dp", None), P(("dp", "tensor"), None)
    columns, grid = P(None, "tensor"), P("dp", "tensor")
    in_specs = (
        (rows, rows, P())
        + (columns,) * 9
        + (P("tensor"), P("tensor"), P(), P("tensor", None), P())
        + (columns, columns, P("tensor", None), both)
    )
    out_specs = (
        (both, both, P())
        + (grid,) * 6
        + (columns,) * 3
        + (P("tensor"), P("tensor"), P(), P("tensor", "dp"), P())
        + (grid, grid, P("tensor", "dp"))
    )
    return jax.shard_map(
        per_device, mesh=mesh, in_specs=in_specs, out_specs=out_specs, check_vma=False
    )
```

```python
import functools

import jax
import jax.numpy as jnp
from jax import lax
from jax.experimental import pallas as pl
from jax.experimental.pallas import tpu as pltpu
from jax.sharding import PartitionSpec as P

CHUNK = 256
EPSILON = 1e-06
F32 = jnp.float32
BF16 = jnp.bfloat16

NN = (((1,), (0,)), ((), ()))
NT = (((1,), (1,)), ((), ()))
TN = (((0,), (0,)), ((), ()))


def low(value):
    return value.astype(BF16)


def mm(left, right, dims):
    return lax.dot_general(left, right, dims, preferred_element_type=F32)


def iotas(rows, columns):
    return (
        lax.broadcasted_iota(jnp.int32, (rows, columns), 0),
        lax.broadcasted_iota(jnp.int32, (rows, columns), 1),
    )


def to_column(row, eye):
    return jnp.sum(jnp.where(eye, row, 0.0), axis=1, keepdims=True)


def to_row(column, eye):
    return jnp.sum(jnp.where(eye, column, 0.0), axis=0, keepdims=True)


def live_masks(segment_column, taps):
    length = segment_column.shape[0]
    wide = jnp.broadcast_to(segment_column, (length, 128))
    rows, _ = iotas(length, 128)
    masks = [None]
    for tap in range(1, taps):
        same = jnp.logical_and(pltpu.roll(wide, tap, 0) == wide, rows >= tap)
        masks.append(jnp.where(same, 1.0, 0.0))
    return masks


def widen(mask, width):
    return jnp.concatenate([mask] * (width // 128), axis=1) if width > 128 else mask


def conv_forward(pre, weight, masks):
    total = pre * weight[0:1]
    for tap in range(1, len(masks)):
        mask = widen(masks[tap], pre.shape[1])
        total = total + pltpu.roll(pre, tap, 0) * mask * weight[tap : tap + 1]
    return total


def conv_backward(upstream, pre, weight, masks):
    length = pre.shape[0]
    back = upstream * weight[0:1]
    weight_rows = [jnp.sum(upstream * pre, axis=0, keepdims=True)]
    for tap in range(1, len(masks)):
        masked = upstream * widen(masks[tap], pre.shape[1])
        back = back + pltpu.roll(masked, length - tap, 0) * weight[tap : tap + 1]
        weight_rows.append(jnp.sum(masked * pltpu.roll(pre, tap, 0), axis=0, keepdims=True))
    return back, jnp.concatenate(weight_rows, axis=0)


def slope(argument, logistic):
    return logistic * (1.0 + argument * (1.0 - logistic))


def unit_rows(values):
    return lax.rsqrt(jnp.sum(values * values, axis=1, keepdims=True) + EPSILON)


def chunk_decays(seg_row, cum_row, at, size, eye):
    rows, cols = iotas(size, size)
    seg = seg_row[:, at : at + size]
    cum = cum_row[:, at : at + size]
    seg_col, cum_col = to_column(seg, eye), to_column(cum, eye)
    keep = jnp.logical_and(rows >= cols, seg_col == seg)
    within = jnp.where(keep, jnp.exp(jnp.where(keep, cum_col - cum, 0.0)), 0.0)
    last_seg, last_cum = seg[:, size - 1 :], cum[:, size - 1 :]
    end = jnp.where(seg_col == last_seg, jnp.exp(last_cum - cum_col), 0.0)
    if at == 0:
        return within, end, None, None
    prev_seg = seg_row[:, at - 1 : at]
    start = jnp.where(seg_col == prev_seg, jnp.exp(cum_col), 0.0)
    carried = jnp.where(last_seg == prev_seg, jnp.exp(last_cum), 0.0)
    return within, end, start, carried


def invert_unit_lower(lower, size):
    rows, cols = iotas(size, size)
    inverse = jnp.where(rows == cols, 1.0, 0.0)
    shift = 0
    while (1 << shift) < size:
        pair = lax.shift_right_logical(rows, shift + 1) == lax.shift_right_logical(cols, shift + 1)
        odd = jnp.bitwise_and(lax.shift_right_logical(rows, shift), 1) == 1
        even = jnp.bitwise_and(lax.shift_right_logical(cols, shift), 1) == 0
        part = jnp.where(jnp.logical_and(pair, jnp.logical_and(odd, even)), lower, 0.0)
        if shift == 0:
            inverse = inverse - part
        else:
            both = low(inverse)
            inverse = inverse - mm(low(mm(both, low(part), NN)), both, NN)
        shift += 1
    return inverse


def forward_kernel(
    chunk, seg_ref, cum_ref, beta_ref, qp_ref, kp_ref, vp_ref, gp_ref, qw_ref, kw_ref, vw_ref,
    og_ref, gated_ref, rec_ref, upd_ref, inv_ref, mem_ref,
):
    length, key_dim = qp_ref.shape
    rows, cols = iotas(chunk, chunk)
    eye = rows == cols
    seg_row, cum_row, beta_row = seg_ref[...], cum_ref[0], beta_ref[0]
    seg_col = jnp.concatenate(
        [to_column(seg_row[:, at : at + chunk], eye) for at in range(0, length, chunk)], axis=0
    )
    masks = live_masks(seg_col, qw_ref.shape[0])

    def silu_conv(pre_ref, weight_ref):
        summed = conv_forward(pre_ref[...], weight_ref[...], masks)
        return summed * jax.nn.sigmoid(summed)

    queries = silu_conv(qp_ref, qw_ref)
    queries = queries * unit_rows(queries) * key_dim ** (-0.5)
    keys = silu_conv(kp_ref, kw_ref)
    keys = keys * unit_rows(keys)
    values = silu_conv(vp_ref, vw_ref)
    gain = og_ref[...]
    memory = None
    for at in range(0, length, chunk):
        here = slice(at, at + chunk)
        within, end, start, carried = chunk_decays(seg_row, cum_row, at, chunk, eye)
        beta = to_column(beta_row[:, here], eye)
        query, key = low(queries[here]), low(keys[here])
        lower = jnp.where(rows > cols, mm(key, key, NT) * within, 0.0) * beta
        inverse = invert_unit_lower(lower, chunk)
        target = values[here]
        if memory is not None:
            mem = low(memory)
            target = target - start * mm(key, mem, NN)
            mem_ref[0, at // chunk * key_dim : (at // chunk + 1) * key_dim, :] = memory
        else:
            mem_ref[0, 0:key_dim, :] = jnp.zeros_like(mem_ref[0, 0:key_dim, :])
        inverse_low = low(inverse)
        upd = low(mm(inverse_low, low(beta * target), NN))
        scores = mm(query, key, NT) * within
        output = mm(low(scores), upd, NN)
        if memory is not None:
            output = output + start * mm(query, mem, NN)
        if at + chunk < length:
            grown = mm(low(keys[here] * end), upd, TN)
            memory = grown if memory is None else carried * memory + grown
        factor = lax.rsqrt(jnp.mean(output * output, axis=1, keepdims=True) + EPSILON)
        gate = gp_ref[here, :]
        gated_ref[here, :] = (
            output * factor * gain * (gate * jax.nn.sigmoid(gate))
        ).astype(BF16)
        rec_ref[here, :] = output
        upd_ref[here, :] = upd
        inv_ref[0, here, :] = inverse_low


def backward_kernel(
    chunk, seg_ref, cum_ref, beta_ref, qp_ref, kp_ref, vp_ref, gp_ref, qw_ref, kw_ref, vw_ref,
    og_ref, rec_ref, upd_ref, inv_ref, mem_ref, up_ref,
    dq_ref, dk_ref, dv_ref, dg_ref, dqw_ref, dkw_ref, dvw_ref, dog_ref, dbeta_ref, dcum_ref,
    query_scr, key_scr, value_scr,
):
    length, key_dim = qp_ref.shape
    scale = key_dim ** (-0.5)
    rows, cols = iotas(chunk, chunk)
    eye = rows == cols
    seg_row, cum_row, beta_row = seg_ref[...], cum_ref[0], beta_ref[0]
    seg_col = jnp.concatenate(
        [to_column(seg_row[:, at : at + chunk], eye) for at in range(0, length, chunk)], axis=0
    )
    masks = live_masks(seg_col, qw_ref.shape[0])
    query_sum = conv_forward(qp_ref[...], qw_ref[...], masks)
    key_sum = conv_forward(kp_ref[...], kw_ref[...], masks)
    value_sum = conv_forward(vp_ref[...], vw_ref[...], masks)
    query_sig, key_sig = jax.nn.sigmoid(query_sum), jax.nn.sigmoid(key_sum)
    value_sig = jax.nn.sigmoid(value_sum)
    query_act, key_act = query_sum * query_sig, key_sum * key_sig
    query_norm, key_norm = unit_rows(query_act), unit_rows(key_act)
    queries = query_act * query_norm * scale
    keys = key_act * key_norm
    values = value_sum * value_sig
    gain = og_ref[...]
    gain_grad = jnp.zeros_like(gain)
    grad_memory = None
    for at in reversed(range(0, length, chunk)):
        here = slice(at, at + chunk)
        index = at // chunk
        output, gate, up = rec_ref[here, :], gp_ref[here, :], up_ref[here, :]
        factor = lax.rsqrt(jnp.mean(output * output, axis=1, keepdims=True) + EPSILON)
        gate_sig = jax.nn.sigmoid(gate)
        normed = output * factor
        silu_gate = gate * gate_sig
        dg_ref[here, :] = (up * normed * gain * slope(gate, gate_sig)).astype(BF16)
        gain_grad = gain_grad + jnp.sum(up * normed * silu_gate, axis=0, keepdims=True)
        weighted = up * gain * silu_gate
        grad_out = factor * (
            weighted - normed * jnp.mean(weighted * normed, axis=1, keepdims=True)
        )
        within, end, start, carried = chunk_decays(seg_row, cum_row, at, chunk, eye)
        beta = to_column(beta_row[:, here], eye)
        query_f, key_f = queries[here], keys[here]
        query, key = low(query_f), low(key_f)
        upd = upd_ref[here, :]
        gram = jnp.where(rows > cols, mm(key, key, NT) * within, 0.0)
        scores = mm(query, key, NT) * within
        grad_o = low(grad_out)
        grad_update = mm(low(scores), grad_o, TN)
        if grad_memory is not None:
            grad_mem = low(grad_memory)
            grad_update = grad_update + mm(low(key_f * end), grad_mem, NN)
        grad_target = mm(inv_ref[0, here, :], low(grad_update), TN)
        grad_scores = mm(grad_o, upd, NT)
        grad_lower = jnp.where(rows > cols, -mm(low(grad_target), upd, NT), 0.0)
        residual = values[here]
        grad_resid = beta * grad_target
        spread = grad_scores * scores + grad_lower * gram * beta
        cum_column = jnp.sum(spread, axis=1, keepdims=True)
        cum_line = -jnp.sum(spread, axis=0, keepdims=True)
        grad_prod = low(grad_scores * within)
        grad_gram = low(grad_lower * within * beta)
        grad_query = mm(grad_prod, key, NN)
        grad_key = mm(grad_prod, query, TN) + mm(grad_gram, key, NN) + mm(grad_gram, key, TN)
        new_grad_memory = None
        if at > 0:
            memory = mem_ref[0, index * key_dim : (index + 1) * key_dim, :]
            mem = low(memory)
            key_mem, query_mem = mm(key, mem, NN), mm(query, mem, NN)
            residual = residual - start * key_mem
            start_out, start_res = start * grad_out, start * grad_resid
            cum_column = cum_column + jnp.sum(
                start_out * query_mem - start_res * key_mem, axis=1, keepdims=True
            )
            start_o, start_r = low(start_out), low(start_res)
            grad_query = grad_query + mm(start_o, mem, NT)
            grad_key = grad_key - mm(start_r, mem, NT)
            new_grad_memory = mm(query, start_o, TN) - mm(key, start_r, TN)
        beta_grad = jnp.sum(grad_target * residual, axis=1, keepdims=True) + jnp.sum(
            grad_lower * gram, axis=1, keepdims=True
        )
        if grad_memory is not None:
            tail = end * mm(upd, grad_mem, NT)
            grad_key = grad_key + tail
            tail_rows = jnp.sum(tail * key_f, axis=1, keepdims=True)
            cum_column = cum_column - tail_rows
            last = jnp.sum(tail_rows, axis=0, keepdims=True)
            if at > 0:
                last = last + carried * jnp.sum(
                    jnp.sum(grad_memory * memory, axis=1, keepdims=True), axis=0, keepdims=True
                )
                new_grad_memory = new_grad_memory + carried * grad_memory
            cum_line = cum_line + jnp.where(cols[0:1] == chunk - 1, last, 0.0)
        grad_memory = new_grad_memory
        dcum_ref[0, :, here] = cum_line + to_row(cum_column, eye)
        dbeta_ref[0, :, here] = to_row(beta_grad, eye)
        query_scr[here, :] = grad_query
        key_scr[here, :] = grad_key
        value_scr[here, :] = grad_resid
    dog_ref[0] = gain_grad
    grad_query, grad_key = query_scr[...], key_scr[...]
    grad_query = (scale * query_norm) * (
        grad_query
        - query_act
        * (query_norm * query_norm * jnp.sum(grad_query * query_act, axis=1, keepdims=True))
    )
    grad_key = key_norm * (
        grad_key
        - key_act * (key_norm * key_norm * jnp.sum(grad_key * key_act, axis=1, keepdims=True))
    )
    back, dqw_ref[...] = conv_backward(
        grad_query * slope(query_sum, query_sig), qp_ref[...], qw_ref[...], masks
    )
    dq_ref[...] = back.astype(BF16)
    back, dkw_ref[...] = conv_backward(
        grad_key * slope(key_sum, key_sig), kp_ref[...], kw_ref[...], masks
    )
    dk_ref[...] = back.astype(BF16)
    back, dvw_ref[...] = conv_backward(
        value_scr[...] * slope(value_sum, value_sig), vp_ref[...], vw_ref[...], masks
    )
    dv_ref[...] = back.astype(BF16)


class Mixer:
    def __init__(self, length, heads, key_dim, value_dim, taps):
        self.chunk = min(CHUNK, length)
        self.length, self.heads = length, heads
        self.key_dim, self.value_dim, self.taps = key_dim, value_dim, taps
        chunks = length // self.chunk
        self.whole = pl.BlockSpec((1, length), lambda h: (0, 0))
        self.line = pl.BlockSpec((1, 1, length), lambda h: (h, 0, 0))
        self.narrow = pl.BlockSpec((length, key_dim), lambda h: (0, h))
        self.wide = pl.BlockSpec((length, value_dim), lambda h: (0, h))
        self.narrow_taps = pl.BlockSpec((taps, key_dim), lambda h: (0, h))
        self.wide_taps = pl.BlockSpec((taps, value_dim), lambda h: (0, h))
        self.gain = pl.BlockSpec((1, value_dim), lambda h: (0, 0))
        self.gain_out = pl.BlockSpec((1, 1, value_dim), lambda h: (h, 0, 0))
        self.inverse = pl.BlockSpec((1, length, self.chunk), lambda h: (h, 0, 0))
        self.memory = pl.BlockSpec((1, chunks * key_dim, value_dim), lambda h: (h, 0, 0))
        self.chunks = chunks
        self.inputs = (
            [self.whole] + [self.line] * 2 + [self.narrow] * 2 + [self.wide] * 2
            + [self.narrow_taps] * 2 + [self.wide_taps, self.gain]
        )
        self.params = pltpu.CompilerParams(
            dimension_semantics=("arbitrary",), vmem_limit_bytes=56 << 20
        )

    def cost(self, products):
        flops = 2 * self.heads * self.chunks * products * self.chunk**3
        return pl.CostEstimate(
            flops=flops,
            transcendentals=self.heads * self.length * 2048,
            bytes_accessed=self.heads * self.length * 1600 * 4,
        )

    def forward(self, *arguments):
        length, heads, values = self.length, self.heads, self.heads * self.value_dim
        return pl.pallas_call(
            functools.partial(forward_kernel, self.chunk),
            grid=(heads,),
            in_specs=self.inputs,
            out_specs=[self.wide] * 3 + [self.inverse, self.memory],
            out_shape=[
                jax.ShapeDtypeStruct((length, values), BF16),
                jax.ShapeDtypeStruct((length, values), F32),
                jax.ShapeDtypeStruct((length, values), BF16),
                jax.ShapeDtypeStruct((heads, length, self.chunk), BF16),
                jax.ShapeDtypeStruct((heads, self.chunks * self.key_dim, self.value_dim), F32),
            ],
            compiler_params=self.params,
            cost_estimate=self.cost(20),
            name="mixer_forward",
        )(*arguments)

    def backward(self, *arguments):
        length, heads = self.length, self.heads
        keys, values = heads * self.key_dim, heads * self.value_dim
        return pl.pallas_call(
            functools.partial(backward_kernel, self.chunk),
            grid=(heads,),
            in_specs=self.inputs + [self.wide] * 2 + [self.inverse, self.memory, self.wide],
            out_specs=[self.narrow] * 2 + [self.wide] * 2 + [self.narrow_taps] * 2
            + [self.wide_taps, self.gain_out] + [self.line] * 2,
            out_shape=[
                jax.ShapeDtypeStruct((length, keys), BF16),
                jax.ShapeDtypeStruct((length, keys), BF16),
                jax.ShapeDtypeStruct((length, values), BF16),
                jax.ShapeDtypeStruct((length, values), BF16),
                jax.ShapeDtypeStruct((self.taps, keys), F32),
                jax.ShapeDtypeStruct((self.taps, keys), F32),
                jax.ShapeDtypeStruct((self.taps, values), F32),
                jax.ShapeDtypeStruct((heads, 1, self.value_dim), F32),
                jax.ShapeDtypeStruct((heads, 1, length), F32),
                jax.ShapeDtypeStruct((heads, 1, length), F32),
            ],
            scratch_shapes=[
                pltpu.VMEM((length, self.key_dim), F32),
                pltpu.VMEM((length, self.key_dim), F32),
                pltpu.VMEM((length, self.value_dim), F32),
            ],
            compiler_params=self.params,
            cost_estimate=self.cost(14),
            name="mixer_backward",
        )(*arguments)


def swapped(value, axis, bit):
    count = lax.axis_size(axis)
    return lax.ppermute(value, axis, [(i, i ^ (1 << bit)) for i in range(count)])


def axis_bits(axis):
    count = lax.axis_size(axis)
    bits = count.bit_length() - 1
    assert count == 1 << bits, "axis size"
    return bits


class Scatter:
    def __init__(self, value, axis, order):
        self.axis, self.order = axis, list(order)
        bits = axis_bits(axis)
        self.left = list(range(bits - 1, -1, -1))
        self.value = value.reshape((2,) * bits + (value.shape[0] >> bits,) + value.shape[1:])

    def step(self):
        bit = self.order.pop(0)
        dim = self.left.index(bit)
        self.left.pop(dim)
        index = lax.axis_index(self.axis)
        mine = jnp.bitwise_and(lax.shift_right_logical(index, bit), 1)
        keep = lax.dynamic_index_in_dim(self.value, mine, dim, keepdims=False)
        send = lax.dynamic_index_in_dim(self.value, 1 - mine, dim, keepdims=False)
        total = keep.astype(F32) + swapped(send, self.axis, bit).astype(F32)
        self.value = total.astype(BF16) if self.order else total

    def finish(self):
        while self.order:
            self.step()
        return self.value.astype(F32)


def scatter_rows(value, axis, order):
    return Scatter(value, axis, order).finish()


def all_sum(value, axis):
    for bit in range(axis_bits(axis)):
        value = value + swapped(value, axis, bit)
    return value


def all_sum_low(value, axis):
    for bit in range(axis_bits(axis)):
        low = value.astype(BF16)
        value = low.astype(F32) + swapped(low, axis, bit).astype(F32)
    return value


def dot(left, right, dims=NN, out=F32):
    return lax.dot_general(left, right, dims, preferred_element_type=out)


def per_device(
    tokens, segment_ids, mixer_gain, query_weight, key_weight, value_weight, gate_weight,
    beta_weight, decay_weight, query_conv, key_conv, value_conv, decay_log, decay_bias,
    output_gain, out_weight, feed_gain, feed_gate, feed_up, feed_down, cotangent,
):
    seq_count, length = segment_ids.shape
    assert seq_count == 1
    heads, value_dim = decay_log.shape[0], output_gain.shape[0]
    key_dim = query_weight.shape[1] // heads
    tensor_bits = axis_bits("tensor")
    tensor_order = list(range(tensor_bits - 1, -1, -1))
    share = length >> tensor_bits
    first_row = lax.axis_index("tensor") * share

    def my_rows(value):
        return lax.dynamic_slice_in_dim(value, first_row, share, 0)

    mixer = Mixer(length, heads, key_dim, value_dim, query_conv.shape[0])
    chunk = mixer.chunk
    cotangent_all = lax.all_gather(cotangent, "tensor", axis=0, tiled=True)
    inputs = tokens.astype(F32)
    factor_first = lax.rsqrt(jnp.mean(inputs * inputs, axis=-1, keepdims=True) + EPSILON)
    normed_in = (inputs * factor_first * mixer_gain).astype(BF16)
    query_pre, key_pre = dot(normed_in, query_weight), dot(normed_in, key_weight)
    value_pre, gate_pre = dot(normed_in, value_weight), dot(normed_in, gate_weight)
    small_weight = jnp.concatenate([beta_weight, decay_weight], axis=1)
    small_pre = dot(small_weight, normed_in, (((0,), (1,)), ((), ())))

    def rates(small, log, bias):
        beta = jax.nn.sigmoid(small[:heads])
        log_decay = -jnp.exp(log)[:, None] * jax.nn.softplus(small[heads:] + bias[:, None])
        upper = jnp.triu(jnp.ones((chunk, chunk), F32))
        summed = lax.dot(
            log_decay.reshape(heads * (length // chunk), chunk), upper,
            precision=lax.Precision.HIGHEST, preferred_element_type=F32,
        )
        return summed.reshape(heads, 1, length), beta.reshape(heads, 1, length)

    (cum, beta), rates_back = jax.vjp(rates, small_pre, decay_log, decay_bias)
    shared = (
        segment_ids.astype(F32), cum, beta, query_pre, key_pre, value_pre, gate_pre,
        query_conv, key_conv, value_conv, output_gain[None],
    )
    gated, recurrent, update, inverse, memory = mixer.forward(*shared)
    middle = inputs + all_sum_low(dot(gated, out_weight), "tensor")
    factor_second = lax.rsqrt(jnp.mean(middle * middle, axis=-1, keepdims=True) + EPSILON)
    normed_mid = (middle * factor_second * feed_gain).astype(BF16)
    swish_in, linear_up = dot(normed_mid, feed_gate), dot(normed_mid, feed_up)
    grad_hidden = dot(cotangent_all, feed_down, NT)
    logistic = jax.nn.sigmoid(swish_in)
    swish = swish_in * logistic
    hidden = (swish * linear_up).astype(BF16)
    swish_grad = (grad_hidden * linear_up * slope(swish_in, logistic)).astype(BF16)
    linear_grad = (grad_hidden * swish).astype(BF16)
    second_part = dot(swish_grad, feed_gate, NT) + dot(linear_grad, feed_up, NT)
    grad_second = all_sum_low(second_part, "tensor")
    feed_part = dot(hidden, feed_down, out=BF16)
    feed_rows = scatter_rows(feed_part, "tensor", tensor_order)
    block_out = (my_rows(middle) + feed_rows).astype(BF16)

    def norm_backward(upstream, values, factor, gain):
        unit = values * factor
        weighted = upstream * gain
        mean = jnp.mean(weighted * unit, axis=-1, keepdims=True)
        return factor * (weighted - unit * mean), upstream * unit

    dp_bits = axis_bits("dp")
    across = [0] + [bit for bit in (1, 2, 3) if bit < dp_bits] + list(range(4, dp_bits))
    along = [0] + list(range(2, dp_bits)) + ([1] if dp_bits > 1 else [])
    if dp_bits == 0:
        across = along = []
    feed_moves = [
        Scatter(dot(normed_mid, swish_grad, TN, BF16), "dp", across),
        Scatter(dot(normed_mid, linear_grad, TN, BF16), "dp", along),
        Scatter(dot(cotangent_all, hidden, TN, BF16), "dp", across),
    ]
    if dp_bits:
        for move in feed_moves:
            move.step()

    back_second, second_terms = norm_backward(grad_second, middle, factor_second, feed_gain)
    gain_second = jnp.sum(my_rows(second_terms), axis=0)
    grad_middle = cotangent_all.astype(F32) + back_second
    grad_middle_low = grad_middle.astype(BF16)
    grad_gated = dot(grad_middle_low, out_weight, NT)
    feed_moves.append(Scatter(dot(grad_middle_low, gated, TN, BF16), "dp", along))
    grad_gated, *values = lax.optimization_barrier(
        [grad_gated] + [move.value for move in feed_moves]
    )
    for move, value in zip(feed_moves, values):
        move.value = value

    (
        low_query, low_key, low_value, low_gate, query_taps, key_taps, value_taps, gain_heads,
        beta_rows, cum_rows,
    ) = mixer.backward(*shared, recurrent, update, inverse, memory, grad_gated)
    small_grad, log_grad, bias_grad = rates_back((cum_rows, beta_rows))
    low_small = small_grad.astype(BF16)
    first_part = (
        dot(low_query, query_weight, NT)
        + dot(low_key, key_weight, NT)
        + dot(low_value, value_weight, NT)
        + dot(low_gate, gate_weight, NT)
        + dot(low_small, small_weight, (((0,), (1,)), ((), ())))
    )
    grad_first = scatter_rows(first_part.astype(BF16), "tensor", tensor_order)
    gate_sum, up_sum, down_sum, out_sum = [move.finish() for move in feed_moves]
    first_move = Scatter(
        dot(normed_in, jnp.concatenate([low_value, low_query], axis=1), TN, BF16), "dp", across
    )
    second_move = Scatter(
        dot(normed_in, jnp.concatenate([low_gate, low_key], axis=1), TN, BF16), "dp", along
    )
    first_sum, second_sum = first_move.finish(), second_move.finish()
    value_count = low_value.shape[1]
    small_part = dot(low_small, normed_in)
    back_first, first_terms = norm_backward(
        grad_first, my_rows(inputs), my_rows(factor_first), mixer_gain
    )
    tokens_grad = (my_rows(grad_middle) + back_first).astype(BF16)

    gains = [jnp.sum(first_terms, axis=0), gain_second, jnp.sum(gain_heads, axis=(0, 1))]
    taps = [query_taps.reshape(-1), key_taps.reshape(-1), value_taps.reshape(-1)]
    own = taps + [log_grad, bias_grad, small_part.reshape(-1)]
    gains_sum = all_sum(jnp.concatenate(gains), "tensor")
    packed = all_sum(jnp.concatenate([gains_sum] + own), "dp")
    sums, place = [], 0
    for piece in gains + own:
        sums.append(packed[place : place + piece.shape[0]])
        place += piece.shape[0]
    small_rows = small_part.shape[1] >> dp_bits
    small_sum = lax.dynamic_slice_in_dim(
        sums[8].reshape(small_part.shape), lax.axis_index("dp") * small_rows, small_rows, 1
    )
    return (
        block_out,
        tokens_grad,
        sums[0],
        first_sum[:, value_count:],
        second_sum[:, value_count:],
        first_sum[:, :value_count],
        second_sum[:, :value_count],
        small_sum[:heads].T,
        small_sum[heads:].T,
        sums[3].reshape(query_conv.shape),
        sums[4].reshape(key_conv.shape),
        sums[5].reshape(value_conv.shape),
        sums[6],
        sums[7],
        sums[2],
        out_sum.T,
        sums[1],
        gate_sum,
        up_sum,
        down_sum.T,
    )


def solution(mesh):
    rows, both = P("dp", None), P(("dp", "tensor"), None)
    columns, grid = P(None, "tensor"), P("dp", "tensor")
    in_specs = (
        (rows, rows, P())
        + (columns,) * 9
        + (P("tensor"), P("tensor"), P(), P("tensor", None), P())
        + (columns, columns, P("tensor", None), both)
    )
    out_specs = (
        (both, both, P())
        + (grid,) * 6
        + (columns,) * 3
        + (P("tensor"), P("tensor"), P(), P("tensor", "dp"), P())
        + (grid, grid, P("tensor", "dp"))
    )
    return jax.shard_map(
        per_device, mesh=mesh, in_specs=in_specs, out_specs=out_specs, check_vma=False
    )
```
